32 devices in a mesh: cube: 2 (over x), chain: 16 (over z, y, core).
Axes of the slice: x: 2, y: 2, z: 4, core: 2. Of those that a mesh axis runs over, the one named last changes fastest.
Arguments:
- conserved: bfloat16 [2, 16, 5, 64, 1024], P('cube', 'chain'), may hold values from -1 to 6, as said below
- element_counts: int32 [2, 16], P('cube', 'chain'), may hold values from 512 to 1024, as said below
- face_links: int32 [2, 16, 4, 1024], P('cube', 'chain'), may hold values from 0 to 1023, as said below
- refinement: int32 [2, 16, 1024], P('cube', 'chain'), may hold values from 0 to 3
- derivative: bfloat16 [3, 64, 64], replicated, may hold values from -0.75 to 0.75
- face_lift: bfloat16 [64, 64], replicated, may hold values from -0.75 to 0.75
Outputs:
- balanced: bfloat16 [2, 16, 5, 64, 1024], P('cube', 'chain')
- balanced_levels: int32 [2, 16, 1024], P('cube', 'chain')
The draws below stay inside these ranges and needn't reach their ends.
Inputs may be any that keep to these rules, and one draw needn't show every extreme that they name: `element_counts`: along cube, every chain index has one device with exactly 1024 live elements and another with exactly 512; live elements fill the slots below the count. `face_links`: each entry names a live slot of the neighbouring device of that face. `conserved`: every node holds a physical state: density and pressure between 0.5 and 2, each velocity component between -0.5 and 0.5.
All inputs are finite; a program needn't handle non-finite values.
Results may differ from the reference program's by a relative error of at most 0.0026.
Values may be sent and summed in bfloat16 or wider, within the bound.
A program may use at most 64 MiB of HBM per device.

```python
import math
import jax
import jax.numpy as jnp
from jax import lax

NODES = 64
FNODES = 16
HOP = 4
SLOTS = 1024
ROUNDS = 1
N_CUBE = 2
N_CHAIN = 16


HEAT_RATIO = 1.4


def load_draw(key):
    folded = jax.random.fold_in(key, 7)
    first_key, second_key, third_key = jax.random.split(folded, 3)
    baseline = jax.random.randint(first_key, (N_CUBE, N_CHAIN), SLOTS // 2, SLOTS // 2 + SLOTS // 8 + 1)
    fullest = jax.random.randint(second_key, (N_CHAIN,), 0, N_CUBE)
    offset = jax.random.randint(third_key, (N_CHAIN,), 1, N_CUBE)
    lightest = (fullest + offset) % N_CUBE
    cube_rows = jnp.arange(N_CUBE, dtype=jnp.int32)[:, None]
    baseline = jnp.where(cube_rows == fullest[None, :], SLOTS, baseline)
    baseline = jnp.where(cube_rows == lightest[None, :], SLOTS // 2, baseline)
    return baseline.astype(jnp.int32)


def draw_element_counts(key, part):
    return load_draw(key)


def draw_face_links(key, part):
    loads = load_draw(key)
    neighbour_loads = jnp.stack([jnp.roll(loads, 1, axis=1), jnp.roll(loads, -1, axis=1), jnp.roll(loads, HOP, axis=1), jnp.roll(loads, -HOP, axis=1)], axis=2)
    random_slot = jax.random.randint(jax.random.fold_in(key, 13), (N_CUBE, N_CHAIN, 4, SLOTS), 0, 1 << 24)
    return (random_slot % neighbour_loads[..., None]).astype(jnp.int32)


def draw_conserved(key, part):
    grid_shape = (N_CUBE, N_CHAIN, NODES, SLOTS)
    subkeys = jax.random.split(jax.random.fold_in(key, 29), 3)
    density = jnp.exp(jax.random.uniform(subkeys[0], grid_shape, jnp.float32, math.log(0.5), math.log(2.0)))
    velocity = jnp.clip(0.2 * jax.random.normal(subkeys[1], (3,) + grid_shape, jnp.float32), -0.5, 0.5)
    pressure = jnp.exp(jax.random.uniform(subkeys[2], grid_shape, jnp.float32, math.log(0.5), math.log(2.0)))
    momenta = density[None] * velocity
    kinetic = velocity[0] * velocity[0] + velocity[1] * velocity[1] + velocity[2] * velocity[2]
    energy = pressure / (HEAT_RATIO - 1.0) + 0.5 * density * kinetic
    fields = jnp.concatenate([density[None], momenta, energy[None]], axis=0)
    return jnp.moveaxis(fields, 0, 2).astype(jnp.bfloat16)


def place_ends(values, key, low, top_value):
    extent = values.shape
    place = [jax.random.randint(jax.random.fold_in(key, axis), (), 0, extent[axis]) for axis in range(len(extent))]
    values = values.at[tuple(place)].set(low)
    longest = extent.index(max(extent))
    place[longest] = (place[longest] + 1) % extent[longest]
    return values.at[tuple(place)].set(top_value)


def gaussian(stream_key, dims, scale, reach, held_as=jnp.bfloat16):
    array = jax.random.normal(stream_key, dims, jnp.float32) * scale
    return jnp.minimum(jnp.maximum(array, -reach), reach).astype(held_as)


def setup_inputs(seed: int = 0) -> dict:
    seeds = jax.random.split(jax.random.key(seed), 7)
    conserved = draw_conserved(jax.random.fold_in(seeds[6], 71), 0)
    element_counts = draw_element_counts(jax.random.fold_in(seeds[6], 71), 0)
    face_links = draw_face_links(jax.random.fold_in(seeds[6], 71), 0)
    refinement = place_ends(jax.random.randint(seeds[3], (N_CUBE, N_CHAIN, SLOTS), 0, 4), jax.random.fold_in(seeds[3], 1), 0, 3).astype(jnp.int32)
    derivative = gaussian(seeds[4], (3, NODES, NODES), NODES ** -0.5, 0.75)
    face_lift = gaussian(seeds[5], (NODES, 4 * FNODES), (4 * FNODES) ** -0.5, 0.75)
    return {"conserved": conserved, "element_counts": element_counts, "face_links": face_links, "refinement": refinement, "derivative": derivative, "face_lift": face_lift}


HEAT_RATIO = 1.4
TIME_STEP = 0.08
FACE_AXES = (2, 2, 1, 1)
FACE_SIGNS = (-1.0, 1.0, -1.0, 1.0)

def flux_along(fields, axis_id):
    density = fields[0]
    momenta = fields[1:4]
    energy = fields[4]
    velocity = momenta[axis_id] / density
    kinetic = momenta[0] * momenta[0] + momenta[1] * momenta[1] + momenta[2] * momenta[2]
    pressure = (HEAT_RATIO - 1.0) * (energy - 0.5 * kinetic / density)
    pieces = [momenta[axis_id]]
    for column in range(3):
        component = momenta[column] * velocity
        if column == axis_id:
            component = component + pressure
        pieces.append(component)
    pieces.append((energy + pressure) * velocity)
    return (jnp.stack(pieces), velocity, pressure)

def face_jump(inner, neighbour, axis_id, orient):
    inner_flux, inner_vel, inner_press = flux_along(inner, axis_id)
    outer_flux, outer_vel, outer_press = flux_along(neighbour, axis_id)
    wave_speed = jnp.maximum(jnp.abs(inner_vel) + jnp.sqrt(HEAT_RATIO * inner_press / inner[0]), jnp.abs(outer_vel) + jnp.sqrt(HEAT_RATIO * outer_press / neighbour[0]))
    return 0.5 * orient * (inner_flux - outer_flux) + 0.5 * wave_speed * (neighbour - inner)

def face_traces(element_block):
    fields_count = element_block.shape[0]
    slot_count = element_block.shape[-1]
    cubed = element_block.reshape(fields_count, 4, 4, 4, slot_count)
    lower_z = cubed[:, 0].reshape(fields_count, 16, slot_count)
    upper_z = cubed[:, 3].reshape(fields_count, 16, slot_count)
    lower_y = cubed[:, :, 0].reshape(fields_count, 16, slot_count)
    upper_y = cubed[:, :, 3].reshape(fields_count, 16, slot_count)
    return (lower_z, upper_z, lower_y, upper_y)

def section_block(element_block, neighbours, level_row, derivative, face_lift):
    inner = element_block.astype(jnp.float32)
    fluxes = jnp.stack([flux_along(inner, axis_id)[0] for axis_id in range(3)]).astype(jnp.bfloat16)
    volume = jnp.einsum('dab,dfbs->fas', derivative.astype(jnp.float32), fluxes.astype(jnp.float32))
    own_faces = face_traces(inner)
    jumps = jnp.concatenate([face_jump(own_faces[face_id], neighbours[face_id].astype(jnp.float32), FACE_AXES[face_id], FACE_SIGNS[face_id]) for face_id in range(4)], axis=1).astype(jnp.bfloat16)
    surface = jnp.einsum('ab,fbs->fas', face_lift.astype(jnp.float32), jumps.astype(jnp.float32))
    factor = (jnp.int32(1) << level_row).astype(jnp.float32)
    return (inner + TIME_STEP * factor * (surface - volume)).astype(jnp.bfloat16)

def rebalance(blocks, loads):
    cube_count = blocks.shape[0]
    slot_count = blocks.shape[-1]
    middle = (1,) * (blocks.ndim - 2)
    position = jnp.arange(slot_count, dtype=jnp.int32)
    members = jnp.arange(cube_count, dtype=jnp.int32)
    for exponent in range(ROUNDS):
        partners = members ^ 1 << exponent
        partner_loads = loads[partners]
        leaving = jnp.maximum(loads - partner_loads, 0) // 2
        arriving = leaving[partners]
        staying = loads - leaving
        source = position[None, :] - staying[:, None] + partner_loads[:, None] - arriving[:, None]
        source = jnp.clip(source, 0, slot_count - 1)
        picks = jnp.broadcast_to(source.reshape((cube_count,) + middle + (slot_count,)), blocks.shape)
        fetched = jnp.take_along_axis(blocks[partners], picks, axis=blocks.ndim - 1)
        kept = (position[None, :] < staying[:, None]).reshape((cube_count,) + middle + (slot_count,))
        window = (position[None, :] < (staying + arriving)[:, None]).reshape((cube_count,) + middle + (slot_count,))
        blocks = jnp.where(kept, blocks, jnp.where(window, fetched, jnp.zeros_like(blocks)))
        loads = staying + arriving
    return blocks

def reference(conserved, element_counts, face_links, refinement, derivative, face_lift):
    cube_count, chain_count, fields_count, node_count, slot_count = conserved.shape
    cubed = conserved.reshape(cube_count, chain_count, fields_count, 4, 4, 4, slot_count)
    lower_z = cubed[:, :, :, 0].reshape(cube_count, chain_count, fields_count, 16, slot_count)
    upper_z = cubed[:, :, :, 3].reshape(cube_count, chain_count, fields_count, 16, slot_count)
    lower_y = cubed[:, :, :, :, 0].reshape(cube_count, chain_count, fields_count, 16, slot_count)
    upper_y = cubed[:, :, :, :, 3].reshape(cube_count, chain_count, fields_count, 16, slot_count)
    sources = (upper_z, lower_z, upper_y, lower_y)
    offsets = (-1, 1, -HOP, HOP)

    def column(chain_at):
        blocks = lax.dynamic_index_in_dim(conserved, chain_at, 1, keepdims=False)
        links_here = lax.dynamic_index_in_dim(face_links, chain_at, 1, keepdims=False)
        neighbours = []
        for face_id in range(4):
            other_chain = (chain_at + offsets[face_id]) % chain_count
            block_faces = lax.dynamic_index_in_dim(sources[face_id], other_chain, 1, keepdims=False)
            picks = jnp.broadcast_to(links_here[:, face_id][:, None, None, :], block_faces.shape)
            neighbours.append(jnp.take_along_axis(block_faces, picks, axis=3))
        level_here = lax.dynamic_index_in_dim(refinement, chain_at, 1, keepdims=False)
        sectioned = jax.vmap(section_block, in_axes=(0, 0, 0, None, None))(blocks, tuple(neighbours), level_here, derivative, face_lift)
        loads = lax.dynamic_index_in_dim(element_counts, chain_at, 1, keepdims=False)
        return (rebalance(sectioned, loads), rebalance(level_here, loads))
    columns, level_columns = lax.map(column, jnp.arange(chain_count, dtype=jnp.int32))
    return (jnp.moveaxis(columns, 0, 1), jnp.moveaxis(level_columns, 0, 1))
```

```python
import functools

import jax
import jax.numpy as jnp
from jax import lax
from jax.experimental import pallas as pl
from jax.experimental.pallas import tpu as pltpu
from jax.sharding import PartitionSpec as P

HOP = 4


HEAT_RATIO = 1.4
TIME_STEP = 0.08
FACE_AXES = (2, 2, 1, 1)
FACE_SIGNS = (-1.0, 1.0, -1.0, 1.0)


def from_partner(block, axis, distance):
    count = lax.axis_size(axis)
    route = []
    for low in range(count):
        high = low | 1 << distance
        if high != low and high < count:
            route += [(low, high), (high, low)]
    return lax.ppermute(block, axis, route)


def send_window(values, staying, capacity):
    slot_count = values.shape[-1]
    start = jnp.minimum(staying, slot_count - capacity)
    return lax.dynamic_slice_in_dim(values, start, capacity, axis=values.ndim - 1)


def land_window(values, received, keep, arriving, partner_staying, capacity):
    slot_axis = values.ndim - 1
    slot_count = values.shape[-1]
    shift = partner_staying - jnp.minimum(partner_staying, slot_count - capacity)
    target = jnp.minimum(keep, slot_count - capacity)
    zero_rows = jnp.zeros(received.shape[:-1] + (capacity,), received.dtype)
    padded = jnp.concatenate([zero_rows, received, zero_rows], axis=slot_axis)
    aligned = lax.dynamic_slice_in_dim(
        padded, capacity + shift - (keep - target), capacity, axis=slot_axis
    )
    position = jnp.arange(slot_count, dtype=jnp.int32)
    kept = jnp.where(position < keep, values, jnp.zeros_like(values))
    region = lax.dynamic_slice_in_dim(kept, target, capacity, axis=slot_axis)
    slot_here = target + jnp.arange(capacity, dtype=jnp.int32)
    update = jnp.where((slot_here >= keep) & (slot_here < keep + arriving), aligned, region)
    return lax.dynamic_update_slice_in_dim(kept, update, target, axis=slot_axis)


def migrate(values, levels, current):
    slot_count = values.shape[-1]
    capacity = slot_count // 4
    rounds_count = lax.axis_size("cube").bit_length() - 1
    for exponent in range(rounds_count):
        partner = from_partner(jnp.reshape(current, (1,)), "cube", exponent)[0]
        leaving = jnp.maximum(current - partner, 0) // 2
        arriving = jnp.maximum(partner - current, 0) // 2
        staying = current - leaving
        partner_staying = partner - arriving
        out_values = send_window(values, staying, capacity)
        out_levels = send_window(levels, staying, capacity)
        in_values, in_levels = from_partner((out_values, out_levels), "cube", exponent)
        values = land_window(values, in_values, staying, arriving, partner_staying, capacity)
        levels = land_window(levels, in_levels, staying, arriving, partner_staying, capacity)
        current = staying + arriving
    return (values, levels, current)


def primitives(w):
    inv = 1.0 / w[0]
    kinetic = w[1] * w[1] + w[2] * w[2] + w[3] * w[3]
    pressure = (HEAT_RATIO - 1.0) * (w[4] - 0.5 * kinetic * inv)
    return inv, pressure


def flux(w, inv, pressure, axis_id):
    momentum = w[1 + axis_id]
    velocity = momentum * inv
    pieces = [momentum]
    for column in range(3):
        component = w[1 + column] * velocity
        if column == axis_id:
            component = component + pressure
        pieces.append(component)
    pieces.append((w[4] + pressure) * velocity)
    return pieces, velocity


def face_jump(inner, neighbour, axis_id, orient):
    inner_inv, inner_press = primitives(inner)
    outer_inv, outer_press = primitives(neighbour)
    inner_flux, inner_vel = flux(inner, inner_inv, inner_press, axis_id)
    outer_flux, outer_vel = flux(neighbour, outer_inv, outer_press, axis_id)
    half_speed = 0.5 * jnp.maximum(
        jnp.abs(inner_vel) + jnp.sqrt(HEAT_RATIO * inner_press * inner_inv),
        jnp.abs(outer_vel) + jnp.sqrt(HEAT_RATIO * outer_press * outer_inv),
    )
    return [
        (0.5 * orient) * (inner_flux[f] - outer_flux[f]) + half_speed * (neighbour[f] - inner[f])
        for f in range(5)
    ]


def section_kernel(
    pairs,
    chain,
    cons,
    links,
    levels,
    counts,
    deriv,
    lift,
    out,
    out_levels,
    ytr,
    nb,
    hot,
    fluxes,
    pre,
    jmp,
    leaving,
    arrived,
    arrived_levels,
    send_sems,
    recv_sems,
):
    slots = cons.shape[-1]
    tile = slots // 4
    c = lax.axis_index("cube")
    h = lax.axis_index("chain")
    ahead = lax.rem(h + 1, chain)
    behind = lax.rem(h + chain - 1, chain)
    hop_ahead = lax.rem(h + HOP, chain)
    hop_behind = lax.rem(h + chain - HOP, chain)
    greet = [(c, ahead), (c, behind), (c, hop_ahead), (c, hop_behind)]
    if pairs:
        greet.append((1 - c, h))
    barrier = pltpu.get_barrier_semaphore()
    for device in greet:
        pl.semaphore_signal(
            barrier, inc=1, device_id=device, device_id_type=pl.DeviceIdType.MESH
        )

    row = lax.broadcasted_iota(jnp.int32, (32, 64), 0)
    col = lax.broadcasted_iota(jnp.int32, (32, 64), 1)
    inside = lax.rem(row, 16)
    node = (inside // 4) * 16 + lax.rem(inside, 4) + jnp.where(row >= 16, 12, 0)
    picker = jnp.where(col == node, 1.0, 0.0).astype(jnp.bfloat16)
    for f in range(5):
        both = jnp.dot(picker, cons[f], preferred_element_type=jnp.float32)
        both = both.astype(jnp.bfloat16)
        ytr[0, f] = both[0:16]
        ytr[1, f] = both[16:32]

    pl.semaphore_wait(barrier, len(greet))

    def send(source, target, index, device):
        copy = pltpu.make_async_remote_copy(
            src_ref=source,
            dst_ref=target,
            send_sem=send_sems.at[index],
            recv_sem=recv_sems.at[index],
            device_id=device,
            device_id_type=pl.DeviceIdType.MESH,
        )
        copy.start()
        return copy

    copies = [None] * 4
    copies[2] = send(ytr.at[1], nb.at[2], 2, (c, hop_ahead))
    copies[3] = send(ytr.at[0], nb.at[3], 3, (c, hop_behind))
    copies[0] = send(cons.at[:, 48:64, :], nb.at[0], 0, (c, ahead))
    copies[1] = send(cons.at[:, 0:16, :], nb.at[1], 1, (c, behind))
    if pairs:
        level_copy = send(levels.at[:, 3 * tile : 4 * tile], arrived_levels, 4, (1 - c, h))

    rows_step = 128
    lanes = lax.broadcasted_iota(jnp.int32, (rows_step, tile), 0)

    def build(face):
        def step(t, carry):
            cols = pl.ds(pl.multiple_of(t * tile, tile), tile)
            link = links[face : face + 1, cols]
            for r in range(0, slots, rows_step):
                hot[face, r : r + rows_step, cols] = jnp.where(
                    lanes == link - r, 1.0, 0.0
                ).astype(jnp.bfloat16)
            return carry

        lax.fori_loop(0, 4, step, 0)

    build(0)
    build(1)

    operator = jnp.concatenate([deriv[0], deriv[1], deriv[2]], axis=1)

    def volume_step(t, carry):
        cols = pl.ds(pl.multiple_of(t * tile, tile), tile)
        for n in range(0, 64, 16):
            w = [cons[f, n : n + 16, cols].astype(jnp.float32) for f in range(5)]
            inv, pressure = primitives(w)
            for d in range(3):
                pieces, _ = flux(w, inv, pressure, d)
                for f in range(5):
                    fluxes[f, 64 * d + n : 64 * d + n + 16, :] = pieces[f].astype(jnp.bfloat16)
        factor = TIME_STEP * (jnp.int32(1) << levels[:, cols]).astype(jnp.float32)
        for f in range(5):
            volume = jnp.dot(operator, fluxes[f], preferred_element_type=jnp.float32)
            pre[f, :, cols] = cons[f, :, cols].astype(jnp.float32) - factor * volume
        return carry

    lax.fori_loop(0, 4, volume_step, 0)
    build(2)
    build(3)

    def jump_tile(face, cols):
        source = nb[face].reshape(80, slots)
        picked = jnp.dot(source, hot[face, :, cols], preferred_element_type=jnp.float32)
        neighbour = [picked[16 * f : 16 * f + 16] for f in range(5)]
        if face == 0:
            inner = [cons[f, 0:16, cols] for f in range(5)]
        elif face == 1:
            inner = [cons[f, 48:64, cols] for f in range(5)]
        else:
            inner = [ytr[face - 2, f, :, cols] for f in range(5)]
        inner = [u.astype(jnp.float32) for u in inner]
        jumps = face_jump(inner, neighbour, FACE_AXES[face], FACE_SIGNS[face])
        for f in range(5):
            jmp[f, 16 * face : 16 * face + 16, cols] = jumps[f].astype(jnp.bfloat16)

    for face in (0, 1):
        copies[face].wait_recv()

        def face_step(t, carry, face=face):
            jump_tile(face, pl.ds(pl.multiple_of(t * tile, tile), tile))
            return carry

        lax.fori_loop(0, 4, face_step, 0)

    copies[2].wait_recv()
    copies[3].wait_recv()
    lifting = lift[...]

    def finish_tile(cols):
        jump_tile(2, cols)
        jump_tile(3, cols)
        factor = TIME_STEP * (jnp.int32(1) << levels[:, cols]).astype(jnp.float32)
        fresh = []
        for f in range(5):
            surface = jnp.dot(lifting, jmp[f, :, cols], preferred_element_type=jnp.float32)
            fresh.append((pre[f, :, cols] + factor * surface).astype(jnp.bfloat16))
        return fresh

    if not pairs:

        def whole_step(t, carry):
            cols = pl.ds(pl.multiple_of(t * tile, tile), tile)
            fresh = finish_tile(cols)
            for f in range(5):
                out[f, :, cols] = fresh[f]
            return carry

        lax.fori_loop(0, 4, whole_step, 0)
        out_levels[...] = levels[...]
        for copy in copies:
            copy.wait_send()
        return

    fresh = finish_tile(pl.ds(3 * tile, tile))
    for f in range(5):
        leaving[f] = fresh[f]
    block_copy = send(leaving, arrived, 5, (1 - c, h))

    def keep_step(t, carry):
        cols = pl.ds(pl.multiple_of(t * tile, tile), tile)
        fresh = finish_tile(cols)
        for f in range(5):
            out[f, :, cols] = fresh[f]
        return carry

    lax.fori_loop(0, 3, keep_step, 0)
    out[:, :, 3 * tile :] = jnp.zeros((5, 64, tile), jnp.bfloat16)

    full = jnp.broadcast_to(counts[0, 0], (1, tile)) == slots
    level_copy.wait_recv()
    out_levels[:, 0 : 2 * tile] = levels[:, 0 : 2 * tile]
    out_levels[:, 2 * tile : 3 * tile] = jnp.where(
        full, levels[:, 2 * tile : 3 * tile], arrived_levels[...]
    )
    out_levels[:, 3 * tile :] = jnp.zeros((1, tile), jnp.int32)
    full_rows = jnp.broadcast_to(counts[0, 0], (64, tile)) == slots
    block_copy.wait_recv()
    for f in range(5):
        out[f, :, 2 * tile : 3 * tile] = jnp.where(
            full_rows,
            out[f, :, 2 * tile : 3 * tile].astype(jnp.float32),
            arrived[f].astype(jnp.float32),
        ).astype(jnp.bfloat16)
    for copy in copies:
        copy.wait_send()
    level_copy.wait_send()
    block_copy.wait_send()


def per_device(conserved, element_counts, face_links, refinement, derivative, face_lift):
    slots = conserved.shape[-1]
    tile = slots // 4
    pairs = lax.axis_size("cube") == 2
    vmem = pl.BlockSpec(memory_space=pltpu.VMEM)
    smem = pl.BlockSpec(memory_space=pltpu.SMEM)
    half = jnp.bfloat16
    fresh, levels = pl.pallas_call(
        functools.partial(section_kernel, pairs, lax.axis_size("chain")),
        out_shape=(
            jax.ShapeDtypeStruct((5, 64, slots), half),
            jax.ShapeDtypeStruct((1, slots), jnp.int32),
        ),
        in_specs=[vmem, vmem, vmem, smem, vmem, vmem],
        out_specs=(vmem, vmem),
        scratch_shapes=[
            pltpu.VMEM((2, 5, 16, slots), half),
            pltpu.VMEM((4, 5, 16, slots), half),
            pltpu.VMEM((4, slots, slots), half),
            pltpu.VMEM((5, 192, tile), half),
            pltpu.VMEM((5, 64, slots), jnp.float32),
            pltpu.VMEM((5, 64, slots), half),
            pltpu.VMEM((5, 64, tile), half),
            pltpu.VMEM((5, 64, tile), half),
            pltpu.VMEM((1, tile), jnp.int32),
            pltpu.SemaphoreType.DMA((6,)),
            pltpu.SemaphoreType.DMA((6,)),
        ],
        compiler_params=pltpu.CompilerParams(
            collective_id=0, has_side_effects=True, vmem_limit_bytes=40 << 20
        ),
    )(conserved[0, 0], face_links[0, 0], refinement[0], element_counts, derivative, face_lift)
    if not pairs:
        fresh, moved, _ = migrate(fresh, levels[0].astype(jnp.bfloat16), element_counts[0, 0])
        levels = moved.astype(jnp.int32)[None]
    return (fresh[None, None], levels[None])


def solution(mesh):
    placed = (
        P("cube", "chain", None, None, None),
        P("cube", "chain"),
        P("cube", "chain", None, None),
        P("cube", "chain", None),
        P(),
        P(),
    )
    return jax.shard_map(
        per_device,
        mesh=mesh,
        in_specs=placed,
        out_specs=(P("cube", "chain", None, None, None), P("cube", "chain", None)),
        check_vma=False,
    )
```

```python
import functools

import jax
import jax.numpy as jnp
from jax import lax
from jax.experimental import pallas as pl
from jax.experimental.pallas import tpu as pltpu
from jax.sharding import PartitionSpec as P

HOP = 4


HEAT_RATIO = 1.4
TIME_STEP = 0.08
FACE_AXES = (2, 2, 1, 1)
FACE_SIGNS = (-1.0, 1.0, -1.0, 1.0)


def from_partner(block, axis, distance):
    count = lax.axis_size(axis)
    route = []
    for low in range(count):
        high = low | 1 << distance
        if high != low and high < count:
            route += [(low, high), (high, low)]
    return lax.ppermute(block, axis, route)


def send_window(values, staying, capacity):
    slot_count = values.shape[-1]
    start = jnp.minimum(staying, slot_count - capacity)
    return lax.dynamic_slice_in_dim(values, start, capacity, axis=values.ndim - 1)


def land_window(values, received, keep, arriving, partner_staying, capacity):
    slot_axis = values.ndim - 1
    slot_count = values.shape[-1]
    shift = partner_staying - jnp.minimum(partner_staying, slot_count - capacity)
    target = jnp.minimum(keep, slot_count - capacity)
    zero_rows = jnp.zeros(received.shape[:-1] + (capacity,), received.dtype)
    padded = jnp.concatenate([zero_rows, received, zero_rows], axis=slot_axis)
    aligned = lax.dynamic_slice_in_dim(
        padded, capacity + shift - (keep - target), capacity, axis=slot_axis
    )
    position = jnp.arange(slot_count, dtype=jnp.int32)
    kept = jnp.where(position < keep, values, jnp.zeros_like(values))
    region = lax.dynamic_slice_in_dim(kept, target, capacity, axis=slot_axis)
    slot_here = target + jnp.arange(capacity, dtype=jnp.int32)
    update = jnp.where((slot_here >= keep) & (slot_here < keep + arriving), aligned, region)
    return lax.dynamic_update_slice_in_dim(kept, update, target, axis=slot_axis)


def migrate(values, levels, current):
    slot_count = values.shape[-1]
    capacity = slot_count // 4
    rounds_count = lax.axis_size("cube").bit_length() - 1
    for exponent in range(rounds_count):
        partner = from_partner(jnp.reshape(current, (1,)), "cube", exponent)[0]
        leaving = jnp.maximum(current - partner, 0) // 2
        arriving = jnp.maximum(partner - current, 0) // 2
        staying = current - leaving
        partner_staying = partner - arriving
        out_values = send_window(values, staying, capacity)
        out_levels = send_window(levels, staying, capacity)
        in_values, in_levels = from_partner((out_values, out_levels), "cube", exponent)
        values = land_window(values, in_values, staying, arriving, partner_staying, capacity)
        levels = land_window(levels, in_levels, staying, arriving, partner_staying, capacity)
        current = staying + arriving
    return (values, levels, current)


def primitives(w):
    inv = 1.0 / w[0]
    kinetic = w[1] * w[1] + w[2] * w[2] + w[3] * w[3]
    pressure = (HEAT_RATIO - 1.0) * (w[4] - 0.5 * kinetic * inv)
    return inv, pressure


def flux(w, inv, pressure, axis_id):
    momentum = w[1 + axis_id]
    velocity = momentum * inv
    pieces = [momentum]
    for column in range(3):
        component = w[1 + column] * velocity
        if column == axis_id:
            component = component + pressure
        pieces.append(component)
    pieces.append((w[4] + pressure) * velocity)
    return pieces, velocity


def face_jump(inner, neighbour, axis_id, orient):
    inner_inv, inner_press = primitives(inner)
    outer_inv, outer_press = primitives(neighbour)
    inner_flux, inner_vel = flux(inner, inner_inv, inner_press, axis_id)
    outer_flux, outer_vel = flux(neighbour, outer_inv, outer_press, axis_id)
    half_speed = 0.5 * jnp.maximum(
        jnp.abs(inner_vel) + jnp.sqrt(HEAT_RATIO * inner_press * inner_inv),
        jnp.abs(outer_vel) + jnp.sqrt(HEAT_RATIO * outer_press * outer_inv),
    )
    return [
        (0.5 * orient) * (inner_flux[f] - outer_flux[f]) + half_speed * (neighbour[f] - inner[f])
        for f in range(5)
    ]


def section_kernel(
    pairs,
    chain,
    cons_hbm,
    links_hbm,
    levels_hbm,
    counts,
    deriv_hbm,
    lift_hbm,
    out,
    out_levels,
    cons,
    links,
    levels,
    deriv,
    lift,
    ytr,
    nb,
    hot,
    fluxes,
    pre,
    jmp,
    moved,
    moved_levels,
    leaving_z,
    leaving_y,
    arrived_z,
    arrived_y,
    load_sems,
    send_sems,
    recv_sems,
):
    slots = cons.shape[-1]
    tile = slots // 4
    c = lax.axis_index("cube")
    h = lax.axis_index("chain")
    ahead = lax.rem(h + 1, chain)
    behind = lax.rem(h + chain - 1, chain)
    hop_ahead = lax.rem(h + HOP, chain)
    hop_behind = lax.rem(h + chain - HOP, chain)
    greet = [(c, ahead), (c, behind), (c, hop_ahead), (c, hop_behind)]
    if pairs:
        greet.append((1 - c, h))
    barrier = pltpu.get_barrier_semaphore()
    for device in greet:
        pl.semaphore_signal(
            barrier, inc=1, device_id=device, device_id_type=pl.DeviceIdType.MESH
        )
    loads = []
    for index, (source, target) in enumerate(
        (
            (cons_hbm, cons),
            (links_hbm, links),
            (levels_hbm, levels),
            (deriv_hbm, deriv),
            (lift_hbm, lift),
        )
    ):
        load = pltpu.make_async_copy(source, target, load_sems.at[index])
        load.start()
        loads.append(load)

    def send(source, target, index, device):
        copy = pltpu.make_async_remote_copy(
            src_ref=source,
            dst_ref=target,
            send_sem=send_sems.at[index],
            recv_sem=recv_sems.at[index],
            device_id=device,
            device_id_type=pl.DeviceIdType.MESH,
        )
        copy.start()
        return copy

    pl.semaphore_wait(barrier, len(greet))
    partner = (1 - c, h)
    copies = [None] * 4
    copies[0] = send(cons_hbm.at[:, 48:64, :], nb.at[0], 0, (c, ahead))
    copies[1] = send(cons_hbm.at[:, 0:16, :], nb.at[1], 1, (c, behind))

    row = lax.broadcasted_iota(jnp.int32, (32, 64), 0)
    col = lax.broadcasted_iota(jnp.int32, (32, 64), 1)
    inside = lax.rem(row, 16)
    node = (inside // 4) * 16 + lax.rem(inside, 4) + jnp.where(row >= 16, 12, 0)
    picker = jnp.where(col == node, 1.0, 0.0).astype(jnp.bfloat16)

    loads[0].wait()
    for f in range(5):
        both = jnp.dot(picker, cons[f], preferred_element_type=jnp.float32)
        both = both.astype(jnp.bfloat16)
        ytr[0, f] = both[0:16]
        ytr[1, f] = both[16:32]

    copies[2] = send(ytr.at[1], nb.at[2], 2, (c, hop_ahead))
    copies[3] = send(ytr.at[0], nb.at[3], 3, (c, hop_behind))
    if pairs:
        moved_copy = send(cons_hbm.at[:, :, 3 * tile :], moved, 4, partner)
        level_copy = send(levels_hbm.at[:, 3 * tile :], moved_levels, 5, partner)

    loads[1].wait()
    rows_step = 128
    lanes = lax.broadcasted_iota(jnp.int32, (rows_step, tile), 0)

    def columns(t):
        return pl.ds(pl.multiple_of(t * tile, tile), tile)

    def build(face):
        def step(t, carry):
            cols = columns(t)
            link = links[face : face + 1, cols]
            for r in range(0, slots, rows_step):
                hot[face, r : r + rows_step, cols] = jnp.where(
                    lanes == link - r, 1.0, 0.0
                ).astype(jnp.bfloat16)
            return carry

        lax.fori_loop(0, 4, step, 0)

    build(0)
    build(1)
    loads[2].wait()
    loads[3].wait()
    loads[4].wait()

    operator = jnp.concatenate([deriv[0], deriv[1], deriv[2]], axis=1)

    def volume_step(t, carry):
        cols = columns(t)
        for n in range(0, 64, 16):
            w = [cons[f, n : n + 16, cols].astype(jnp.float32) for f in range(5)]
            inv, pressure = primitives(w)
            for d in range(3):
                pieces, _ = flux(w, inv, pressure, d)
                for f in range(5):
                    fluxes[f, 64 * d + n : 64 * d + n + 16, :] = pieces[f].astype(jnp.bfloat16)
        factor = TIME_STEP * (jnp.int32(1) << levels[:, cols]).astype(jnp.float32)
        for f in range(5):
            volume = jnp.dot(operator, fluxes[f], preferred_element_type=jnp.float32)
            pre[f, :, cols] = cons[f, :, cols].astype(jnp.float32) - factor * volume
        return carry

    def jump_tile(face, cols, target, first, target_cols):
        source = nb[face].reshape(80, slots)
        picked = jnp.dot(source, hot[face, :, cols], preferred_element_type=jnp.float32)
        neighbour = [picked[16 * f : 16 * f + 16] for f in range(5)]
        if face == 0:
            inner = [cons[f, 0:16, cols] for f in range(5)]
        elif face == 1:
            inner = [cons[f, 48:64, cols] for f in range(5)]
        else:
            inner = [ytr[face - 2, f, :, cols] for f in range(5)]
        inner = [u.astype(jnp.float32) for u in inner]
        jumps = face_jump(inner, neighbour, FACE_AXES[face], FACE_SIGNS[face])
        for f in range(5):
            target[f, first : first + 16, target_cols] = jumps[f].astype(jnp.bfloat16)

    def keep_jumps(face, count):
        def step(t, carry):
            cols = columns(t)
            jump_tile(face, cols, jmp, 16 * face, cols)
            return carry

        lax.fori_loop(0, count, step, 0)

    def finish(cols):
        factor = TIME_STEP * (jnp.int32(1) << levels[:, cols]).astype(jnp.float32)
        for f in range(5):
            surface = jnp.dot(lift[...], jmp[f, :, cols], preferred_element_type=jnp.float32)
            out[f, :, cols] = (pre[f, :, cols] + factor * surface).astype(jnp.bfloat16)

    if not pairs:
        build(2)
        build(3)
        lax.fori_loop(0, 4, volume_step, 0)
        for face in range(4):
            copies[face].wait_recv()
            keep_jumps(face, 4)

        def whole_step(t, carry):
            finish(columns(t))
            return carry

        lax.fori_loop(0, 4, whole_step, 0)
        out_levels[...] = levels[...]
        for copy in copies:
            copy.wait_send()
        return

    last = pl.ds(3 * tile, tile)
    third = pl.ds(2 * tile, tile)
    here = pl.ds(0, tile)
    for face in (0, 1):
        copies[face].wait_recv()
        jump_tile(face, last, leaving_z, 16 * face, here)
    z_copy = send(leaving_z, arrived_z, 6, partner)
    build(2)
    build(3)
    keep_jumps(0, 3)
    keep_jumps(1, 3)
    lax.fori_loop(0, 2, volume_step, 0)

    def choose(own, other):
        full = jnp.broadcast_to(counts[0, 0], own.shape) == slots
        chosen = jnp.where(full, own.astype(jnp.float32), other.astype(jnp.float32))
        return chosen.astype(own.dtype)

    level_copy.wait_recv()
    full = jnp.broadcast_to(counts[0, 0], (1, tile)) == slots
    out_levels[:, 0 : 2 * tile] = levels[:, 0 : 2 * tile]
    chosen_levels = jnp.where(full, levels[:, third], moved_levels[...])
    out_levels[:, third] = chosen_levels
    out_levels[:, last] = jnp.zeros((1, tile), jnp.int32)
    factor = TIME_STEP * (jnp.int32(1) << chosen_levels).astype(jnp.float32)
    moved_copy.wait_recv()
    for n in range(0, 64, 16):
        w = []
        for f in range(5):
            own = cons[f, n : n + 16, third]
            chosen = choose(own, moved[f, n : n + 16, :])
            pre[f, n : n + 16, third] = chosen.astype(jnp.float32)
            w.append(chosen.astype(jnp.float32))
        inv, pressure = primitives(w)
        for d in range(3):
            pieces, _ = flux(w, inv, pressure, d)
            for f in range(5):
                fluxes[f, 64 * d + n : 64 * d + n + 16, :] = pieces[f].astype(jnp.bfloat16)
    for f in range(5):
        volume = jnp.dot(operator, fluxes[f], preferred_element_type=jnp.float32)
        pre[f, :, third] = pre[f, :, third] - factor * volume
    z_copy.wait_recv()
    for f in range(5):
        jmp[f, 0:32, third] = choose(jmp[f, 0:32, third], arrived_z[f])
    out[:, :, last] = jnp.zeros((5, 64, tile), jnp.bfloat16)

    y_copies = []
    for face in (2, 3):
        copies[face].wait_recv()
        side = leaving_y.at[face - 2]
        jump_tile(face, last, side, 0, here)
        y_copies.append(send(side, arrived_y.at[face - 2], 5 + face, partner))
    for face in (2, 3):
        keep_jumps(face, 3)

    def keep_step(t, carry):
        finish(columns(t))
        return carry

    lax.fori_loop(0, 2, keep_step, 0)
    for face in (2, 3):
        y_copies[face - 2].wait_recv()
        for f in range(5):
            own = jmp[f, 16 * face : 16 * face + 16, third]
            jmp[f, 16 * face : 16 * face + 16, third] = choose(own, arrived_y[face - 2, f])
    for f in range(5):
        surface = jnp.dot(lift[...], jmp[f, :, third], preferred_element_type=jnp.float32)
        out[f, :, third] = (pre[f, :, third] + factor * surface).astype(jnp.bfloat16)
    for copy in copies + y_copies + [moved_copy, level_copy, z_copy]:
        copy.wait_send()


def stay(block):
    return pltpu.with_memory_space_constraint(block, pltpu.HBM)


def per_device(conserved, element_counts, face_links, refinement, derivative, face_lift):
    slots = conserved.shape[-1]
    tile = slots // 4
    pairs = lax.axis_size("cube") == 2
    vmem = pl.BlockSpec(memory_space=pltpu.VMEM)
    hbm = pl.BlockSpec(memory_space=pltpu.HBM)
    smem = pl.BlockSpec(memory_space=pltpu.SMEM)
    half = jnp.bfloat16
    fresh, levels = pl.pallas_call(
        functools.partial(section_kernel, pairs, lax.axis_size("chain")),
        out_shape=(
            jax.ShapeDtypeStruct((5, 64, slots), half),
            jax.ShapeDtypeStruct((1, slots), jnp.int32),
        ),
        in_specs=[hbm, hbm, hbm, smem, hbm, hbm],
        out_specs=(vmem, vmem),
        scratch_shapes=[
            pltpu.VMEM((5, 64, slots), half),
            pltpu.VMEM((4, slots), jnp.int32),
            pltpu.VMEM((1, slots), jnp.int32),
            pltpu.VMEM((3, 64, 64), half),
            pltpu.VMEM((64, 64), half),
            pltpu.VMEM((2, 5, 16, slots), half),
            pltpu.VMEM((4, 5, 16, slots), half),
            pltpu.VMEM((4, slots, slots), half),
            pltpu.VMEM((5, 192, tile), half),
            pltpu.VMEM((5, 64, slots), jnp.float32),
            pltpu.VMEM((5, 64, slots), half),
            pltpu.VMEM((5, 64, tile), half),
            pltpu.VMEM((1, tile), jnp.int32),
            pltpu.VMEM((5, 32, tile), half),
            pltpu.VMEM((2, 5, 16, tile), half),
            pltpu.VMEM((5, 32, tile), half),
            pltpu.VMEM((2, 5, 16, tile), half),
            pltpu.SemaphoreType.DMA((5,)),
            pltpu.SemaphoreType.DMA((9,)),
            pltpu.SemaphoreType.DMA((9,)),
        ],
        compiler_params=pltpu.CompilerParams(
            collective_id=0, has_side_effects=True, vmem_limit_bytes=40 << 20
        ),
    )(
        stay(conserved[0, 0]),
        stay(face_links[0, 0]),
        stay(refinement[0]),
        element_counts,
        stay(derivative),
        stay(face_lift),
    )
    if not pairs:
        fresh, moved, _ = migrate(fresh, levels[0].astype(jnp.bfloat16), element_counts[0, 0])
        levels = moved.astype(jnp.int32)[None]
    return (fresh[None, None], levels[None])


def solution(mesh):
    placed = (
        P("cube", "chain", None, None, None),
        P("cube", "chain"),
        P("cube", "chain", None, None),
        P("cube", "chain", None),
        P(),
        P(),
    )
    return jax.shard_map(
        per_device,
        mesh=mesh,
        in_specs=placed,
        out_specs=(P("cube", "chain", None, None, None), P("cube", "chain", None)),
        check_vma=False,
    )
```

```python
import functools

import jax
import jax.numpy as jnp
from jax import lax
from jax.experimental import pallas as pl
from jax.experimental.pallas import tpu as pltpu
from jax.sharding import PartitionSpec as P

HOP = 4


HEAT_RATIO = 1.4
TIME_STEP = 0.08
FACE_AXES = (2, 2, 1, 1)
FACE_SIGNS = (-1.0, 1.0, -1.0, 1.0)


def from_partner(block, axis, distance):
    count = lax.axis_size(axis)
    route = []
    for low in range(count):
        high = low | 1 << distance
        if high != low and high < count:
            route += [(low, high), (high, low)]
    return lax.ppermute(block, axis, route)


def send_window(values, staying, capacity):
    slot_count = values.shape[-1]
    start = jnp.minimum(staying, slot_count - capacity)
    return lax.dynamic_slice_in_dim(values, start, capacity, axis=values.ndim - 1)


def land_window(values, received, keep, arriving, partner_staying, capacity):
    slot_axis = values.ndim - 1
    slot_count = values.shape[-1]
    shift = partner_staying - jnp.minimum(partner_staying, slot_count - capacity)
    target = jnp.minimum(keep, slot_count - capacity)
    zero_rows = jnp.zeros(received.shape[:-1] + (capacity,), received.dtype)
    padded = jnp.concatenate([zero_rows, received, zero_rows], axis=slot_axis)
    aligned = lax.dynamic_slice_in_dim(
        padded, capacity + shift - (keep - target), capacity, axis=slot_axis
    )
    position = jnp.arange(slot_count, dtype=jnp.int32)
    kept = jnp.where(position < keep, values, jnp.zeros_like(values))
    region = lax.dynamic_slice_in_dim(kept, target, capacity, axis=slot_axis)
    slot_here = target + jnp.arange(capacity, dtype=jnp.int32)
    update = jnp.where((slot_here >= keep) & (slot_here < keep + arriving), aligned, region)
    return lax.dynamic_update_slice_in_dim(kept, update, target, axis=slot_axis)


def migrate(values, levels, current):
    slot_count = values.shape[-1]
    capacity = slot_count // 4
    rounds_count = lax.axis_size("cube").bit_length() - 1
    for exponent in range(rounds_count):
        partner = from_partner(jnp.reshape(current, (1,)), "cube", exponent)[0]
        leaving = jnp.maximum(current - partner, 0) // 2
        arriving = jnp.maximum(partner - current, 0) // 2
        staying = current - leaving
        partner_staying = partner - arriving
        out_values = send_window(values, staying, capacity)
        out_levels = send_window(levels, staying, capacity)
        in_values, in_levels = from_partner((out_values, out_levels), "cube", exponent)
        values = land_window(values, in_values, staying, arriving, partner_staying, capacity)
        levels = land_window(levels, in_levels, staying, arriving, partner_staying, capacity)
        current = staying + arriving
    return (values, levels, current)


def primitives(w):
    inv = 1.0 / w[0]
    kinetic = w[1] * w[1] + w[2] * w[2] + w[3] * w[3]
    pressure = (HEAT_RATIO - 1.0) * (w[4] - 0.5 * kinetic * inv)
    return inv, pressure


def flux(w, inv, pressure, axis_id):
    momentum = w[1 + axis_id]
    velocity = momentum * inv
    pieces = [momentum]
    for column in range(3):
        component = w[1 + column] * velocity
        if column == axis_id:
            component = component + pressure
        pieces.append(component)
    pieces.append((w[4] + pressure) * velocity)
    return pieces, velocity


def face_jump(inner, neighbour, axis_id, orient):
    inner_inv, inner_press = primitives(inner)
    outer_inv, outer_press = primitives(neighbour)
    inner_flux, inner_vel = flux(inner, inner_inv, inner_press, axis_id)
    outer_flux, outer_vel = flux(neighbour, outer_inv, outer_press, axis_id)
    half_speed = 0.5 * jnp.maximum(
        jnp.abs(inner_vel) + jnp.sqrt(HEAT_RATIO * inner_press * inner_inv),
        jnp.abs(outer_vel) + jnp.sqrt(HEAT_RATIO * outer_press * outer_inv),
    )
    return [
        (0.5 * orient) * (inner_flux[f] - outer_flux[f]) + half_speed * (neighbour[f] - inner[f])
        for f in range(5)
    ]


def section_kernel(
    pairs,
    chain,
    cons_hbm,
    links_hbm,
    levels_hbm,
    counts,
    deriv_hbm,
    lift_hbm,
    out,
    out_levels,
    cons,
    links,
    levels,
    deriv,
    lift,
    ytr,
    nb,
    hot,
    fluxes,
    pre,
    jmp,
    moved,
    moved_levels,
    leaving_z,
    leaving_y,
    arrived_z,
    arrived_y,
    load_sems,
    send_sems,
    recv_sems,
):
    slots = cons.shape[-1]
    tile = slots // 4
    c = lax.axis_index("cube")
    h = lax.axis_index("chain")
    ahead = lax.rem(h + 1, chain)
    behind = lax.rem(h + chain - 1, chain)
    hop_ahead = lax.rem(h + HOP, chain)
    hop_behind = lax.rem(h + chain - HOP, chain)
    greet = [(c, ahead), (c, behind), (c, hop_ahead), (c, hop_behind)]
    if pairs:
        greet.append((1 - c, h))
    barrier = pltpu.get_barrier_semaphore()
    for device in greet:
        pl.semaphore_signal(
            barrier, inc=1, device_id=device, device_id_type=pl.DeviceIdType.MESH
        )
    fields = []
    for f in range(5):
        load = pltpu.make_async_copy(cons_hbm.at[f], cons.at[f], load_sems.at[4 + f])
        load.start()
        fields.append(load)
    loads = [None]
    for index, (source, target) in enumerate(
        (
            (links_hbm, links),
            (levels_hbm, levels),
            (deriv_hbm, deriv),
            (lift_hbm, lift),
        )
    ):
        load = pltpu.make_async_copy(source, target, load_sems.at[index])
        load.start()
        loads.append(load)

    def send(source, target, index, device):
        copy = pltpu.make_async_remote_copy(
            src_ref=source,
            dst_ref=target,
            send_sem=send_sems.at[index],
            recv_sem=recv_sems.at[index],
            device_id=device,
            device_id_type=pl.DeviceIdType.MESH,
        )
        copy.start()
        return copy

    pl.semaphore_wait(barrier, len(greet))
    partner = (1 - c, h)
    copies = [None] * 4
    copies[0] = send(cons_hbm.at[:, 48:64, :], nb.at[0], 0, (c, ahead))
    copies[1] = send(cons_hbm.at[:, 0:16, :], nb.at[1], 1, (c, behind))

    row = lax.broadcasted_iota(jnp.int32, (32, 64), 0)
    col = lax.broadcasted_iota(jnp.int32, (32, 64), 1)
    inside = lax.rem(row, 16)
    node = (inside // 4) * 16 + lax.rem(inside, 4) + jnp.where(row >= 16, 12, 0)
    picker = jnp.where(col == node, 1.0, 0.0).astype(jnp.bfloat16)

    for f in range(5):
        fields[f].wait()
        both = jnp.dot(picker, cons[f], preferred_element_type=jnp.float32)
        both = both.astype(jnp.bfloat16)
        ytr[0, f] = both[0:16]
        ytr[1, f] = both[16:32]

    copies[2] = send(ytr.at[1], nb.at[2], 2, (c, hop_ahead))
    copies[3] = send(ytr.at[0], nb.at[3], 3, (c, hop_behind))
    if pairs:
        moved_copy = send(cons_hbm.at[:, :, 3 * tile :], moved, 4, partner)
        level_copy = send(levels_hbm.at[:, 3 * tile :], moved_levels, 5, partner)

    loads[1].wait()
    rows_step = 128
    lanes = lax.broadcasted_iota(jnp.int32, (rows_step, tile), 0)

    def columns(t):
        return pl.ds(pl.multiple_of(t * tile, tile), tile)

    def build(face):
        def step(t, carry):
            cols = columns(t)
            link = links[face : face + 1, cols]
            for r in range(0, slots, rows_step):
                hot[face, r : r + rows_step, cols] = jnp.where(
                    lanes == link - r, 1.0, 0.0
                ).astype(jnp.bfloat16)
            return carry

        lax.fori_loop(0, 4, step, 0)

    build(0)
    build(1)
    loads[2].wait()
    loads[3].wait()
    loads[4].wait()

    operator = jnp.concatenate([deriv[0], deriv[1], deriv[2]], axis=1)

    def volume_step(t, carry):
        cols = columns(t)
        for n in range(0, 64, 16):
            w = [cons[f, n : n + 16, cols].astype(jnp.float32) for f in range(5)]
            inv, pressure = primitives(w)
            for d in range(3):
                pieces, _ = flux(w, inv, pressure, d)
                for f in range(5):
                    fluxes[f, 64 * d + n : 64 * d + n + 16, :] = pieces[f].astype(jnp.bfloat16)
        factor = TIME_STEP * (jnp.int32(1) << levels[:, cols]).astype(jnp.float32)
        for f in range(5):
            volume = jnp.dot(operator, fluxes[f], preferred_element_type=jnp.float32)
            pre[f, :, cols] = cons[f, :, cols].astype(jnp.float32) - factor * volume
        return carry

    def jump_tile(face, cols, target, first, target_cols):
        source = nb[face].reshape(80, slots)
        picked = jnp.dot(source, hot[face, :, cols], preferred_element_type=jnp.float32)
        neighbour = [picked[16 * f : 16 * f + 16] for f in range(5)]
        if face == 0:
            inner = [cons[f, 0:16, cols] for f in range(5)]
        elif face == 1:
            inner = [cons[f, 48:64, cols] for f in range(5)]
        else:
            inner = [ytr[face - 2, f, :, cols] for f in range(5)]
        inner = [u.astype(jnp.float32) for u in inner]
        jumps = face_jump(inner, neighbour, FACE_AXES[face], FACE_SIGNS[face])
        for f in range(5):
            target[f, first : first + 16, target_cols] = jumps[f].astype(jnp.bfloat16)

    def keep_jumps(face, count):
        def step(t, carry):
            cols = columns(t)
            jump_tile(face, cols, jmp, 16 * face, cols)
            return carry

        lax.fori_loop(0, count, step, 0)

    def finish(cols):
        factor = TIME_STEP * (jnp.int32(1) << levels[:, cols]).astype(jnp.float32)
        for f in range(5):
            surface = jnp.dot(lift[...], jmp[f, :, cols], preferred_element_type=jnp.float32)
            out[f, :, cols] = (pre[f, :, cols] + factor * surface).astype(jnp.bfloat16)

    if not pairs:
        build(2)
        build(3)
        lax.fori_loop(0, 4, volume_step, 0)
        for face in range(4):
            copies[face].wait_recv()
            keep_jumps(face, 4)

        def whole_step(t, carry):
            finish(columns(t))
            return carry

        lax.fori_loop(0, 4, whole_step, 0)
        out_levels[...] = levels[...]
        for copy in copies:
            copy.wait_send()
        return

    last = pl.ds(3 * tile, tile)
    third = pl.ds(2 * tile, tile)
    here = pl.ds(0, tile)
    for face in (0, 1):
        copies[face].wait_recv()
        jump_tile(face, last, leaving_z, 16 * face, here)
    z_copy = send(leaving_z, arrived_z, 6, partner)
    build(2)
    build(3)
    keep_jumps(0, 3)
    keep_jumps(1, 3)
    lax.fori_loop(0, 2, volume_step, 0)

    def choose(own, other):
        full = jnp.broadcast_to(counts[0, 0], own.shape) == slots
        chosen = jnp.where(full, own.astype(jnp.float32), other.astype(jnp.float32))
        return chosen.astype(own.dtype)

    level_copy.wait_recv()
    full = jnp.broadcast_to(counts[0, 0], (1, tile)) == slots
    out_levels[:, 0 : 2 * tile] = levels[:, 0 : 2 * tile]
    chosen_levels = jnp.where(full, levels[:, third], moved_levels[...])
    out_levels[:, third] = chosen_levels
    out_levels[:, last] = jnp.zeros((1, tile), jnp.int32)
    factor = TIME_STEP * (jnp.int32(1) << chosen_levels).astype(jnp.float32)
    moved_copy.wait_recv()
    for n in range(0, 64, 16):
        w = []
        for f in range(5):
            own = cons[f, n : n + 16, third]
            chosen = choose(own, moved[f, n : n + 16, :])
            pre[f, n : n + 16, third] = chosen.astype(jnp.float32)
            w.append(chosen.astype(jnp.float32))
        inv, pressure = primitives(w)
        for d in range(3):
            pieces, _ = flux(w, inv, pressure, d)
            for f in range(5):
                fluxes[f, 64 * d + n : 64 * d + n + 16, :] = pieces[f].astype(jnp.bfloat16)
    for f in range(5):
        volume = jnp.dot(operator, fluxes[f], preferred_element_type=jnp.float32)
        pre[f, :, third] = pre[f, :, third] - factor * volume
    z_copy.wait_recv()
    for f in range(5):
        jmp[f, 0:32, third] = choose(jmp[f, 0:32, third], arrived_z[f])
    out[:, :, last] = jnp.zeros((5, 64, tile), jnp.bfloat16)

    y_copies = []
    for face in (2, 3):
        copies[face].wait_recv()
        side = leaving_y.at[face - 2]
        jump_tile(face, last, side, 0, here)
        y_copies.append(send(side, arrived_y.at[face - 2], 5 + face, partner))
    for face in (2, 3):
        keep_jumps(face, 3)

    def keep_step(t, carry):
        finish(columns(t))
        return carry

    lax.fori_loop(0, 2, keep_step, 0)
    for face in (2, 3):
        y_copies[face - 2].wait_recv()
        for f in range(5):
            own = jmp[f, 16 * face : 16 * face + 16, third]
            jmp[f, 16 * face : 16 * face + 16, third] = choose(own, arrived_y[face - 2, f])
    for f in range(5):
        surface = jnp.dot(lift[...], jmp[f, :, third], preferred_element_type=jnp.float32)
        out[f, :, third] = (pre[f, :, third] + factor * surface).astype(jnp.bfloat16)
    for copy in copies + y_copies + [moved_copy, level_copy, z_copy]:
        copy.wait_send()


def stay(block):
    return pltpu.with_memory_space_constraint(block, pltpu.HBM)


def per_device(conserved, element_counts, face_links, refinement, derivative, face_lift):
    slots = conserved.shape[-1]
    tile = slots // 4
    pairs = lax.axis_size("cube") == 2
    vmem = pl.BlockSpec(memory_space=pltpu.VMEM)
    hbm = pl.BlockSpec(memory_space=pltpu.HBM)
    smem = pl.BlockSpec(memory_space=pltpu.SMEM)
    half = jnp.bfloat16
    fresh, levels = pl.pallas_call(
        functools.partial(section_kernel, pairs, lax.axis_size("chain")),
        out_shape=(
            jax.ShapeDtypeStruct((5, 64, slots), half),
            jax.ShapeDtypeStruct((1, slots), jnp.int32),
        ),
        in_specs=[hbm, hbm, hbm, smem, hbm, hbm],
        out_specs=(vmem, vmem),
        scratch_shapes=[
            pltpu.VMEM((5, 64, slots), half),
            pltpu.VMEM((4, slots), jnp.int32),
            pltpu.VMEM((1, slots), jnp.int32),
            pltpu.VMEM((3, 64, 64), half),
            pltpu.VMEM((64, 64), half),
            pltpu.VMEM((2, 5, 16, slots), half),
            pltpu.VMEM((4, 5, 16, slots), half),
            pltpu.VMEM((4, slots, slots), half),
            pltpu.VMEM((5, 192, tile), half),
            pltpu.VMEM((5, 64, slots), jnp.float32),
            pltpu.VMEM((5, 64, slots), half),
            pltpu.VMEM((5, 64, tile), half),
            pltpu.VMEM((1, tile), jnp.int32),
            pltpu.VMEM((5, 32, tile), half),
            pltpu.VMEM((2, 5, 16, tile), half),
            pltpu.VMEM((5, 32, tile), half),
            pltpu.VMEM((2, 5, 16, tile), half),
            pltpu.SemaphoreType.DMA((9,)),
            pltpu.SemaphoreType.DMA((9,)),
            pltpu.SemaphoreType.DMA((9,)),
        ],
        compiler_params=pltpu.CompilerParams(
            collective_id=0, has_side_effects=True, vmem_limit_bytes=40 << 20
        ),
    )(
        stay(conserved[0, 0]),
        stay(face_links[0, 0]),
        stay(refinement[0]),
        element_counts,
        stay(derivative),
        stay(face_lift),
    )
    if not pairs:
        fresh, moved, _ = migrate(fresh, levels[0].astype(jnp.bfloat16), element_counts[0, 0])
        levels = moved.astype(jnp.int32)[None]
    return (fresh[None, None], levels[None])


def solution(mesh):
    placed = (
        P("cube", "chain", None, None, None),
        P("cube", "chain"),
        P("cube", "chain", None, None),
        P("cube", "chain", None),
        P(),
        P(),
    )
    return jax.shard_map(
        per_device,
        mesh=mesh,
        in_specs=placed,
        out_specs=(P("cube", "chain", None, None, None), P("cube", "chain", None)),
        check_vma=False,
    )
```
